32 devices in a mesh: dp: 8 (over z, x), ctx: 4 (over y, core).
Axes of the slice: x: 2, y: 2, z: 4, core: 2. Of those that a mesh axis runs over, the one named last changes fastest.
Arguments:
- tokens: bfloat16 [8, 1, 1024, 2560], P('dp', None, 'ctx'), may hold values from -6 to 6
- target: bfloat16 [8, 1, 1024, 2560], P('dp', None, 'ctx'), may hold values from -6 to 6
- rewards: float32 [8, 1, 1024], P('dp', None, 'ctx'), may hold values from 0.25 to 4
- doc_lengths: int32 [8, 1, 4], P('dp'), may hold values from 1 to 512, 1024 in all within a row
- norm_gain: float32 [2560], replicated, may hold values from 0.1 to 1.9
- w_query: bfloat16 [2560, 1024], P(('dp', 'ctx')), as said below
- w_key: bfloat16 [2560, 512], P(('dp', 'ctx')), as said below
- w_value: bfloat16 [2560, 512], P(('dp', 'ctx')), may hold values from -0.125 to 0.125
- w_out: bfloat16 [1024, 2560], P(('dp', 'ctx')), may hold values from -0.1875 to 0.1875
- gossip_bit: int32 [8], P('dp'), may hold values from 0 to 2, as said below
Outputs:
- grad_query: float32 [8, 2560, 1024], P('dp', 'ctx')
- grad_key: float32 [8, 2560, 512], P('dp', 'ctx')
- grad_value: float32 [8, 2560, 512], P('dp', 'ctx')
- grad_out: float32 [8, 1024, 2560], P('dp', 'ctx')
The draws below stay inside these ranges and needn't reach their ends.
Inputs may be any that keep to these rules, and one draw needn't show every extreme that they name: `doc_lengths`: the lengths of one sequence sum to 1024; the longest is exactly 512. `gossip_bit`: every bit from 0 to 2 is named by some group. `w_query`: a projection's weights. `w_key`: a projection's weights.
All inputs are finite; a program needn't handle non-finite values.
Results may differ from the reference program's by a relative error of at most 0.019.
The reference program's roundings to bfloat16 on the way count: a program that leaves them out, or rounds other values in their place, can miss the bound.
Values may be sent and summed in bfloat16 or wider, within the bound.
No kernel may reach another device: no remote copies, remote signals or barrier semaphores. Data moves between devices by JAX's collectives and lax.ppermute only.
A program may use at most 128 MiB of HBM per device.

```python
import math
import jax
import jax.numpy as jnp
import numpy as np
from jax import lax

MODEL_DIM = 2560
QUERY_HEADS = 4
KEY_VALUE_HEADS = 2
HEAD_DIM = 256
WINDOW = 1024
TOK_DEV = 256
SEQ_DEV = 1
QW = 1024
KW = 512
LENGTH = 1024
DOCS = 4
MOST_DOC = 512
GOSSIP_LEVELS = 3
N_DP = 8
N_CTX = 4


def shared_weights(key):
    query_key = jax.random.fold_in(key, 11)
    local_key = jax.random.fold_in(key, 12)
    query_matrix = jnp.clip(jax.random.normal(query_key, (MODEL_DIM, QUERY_HEADS * HEAD_DIM), jnp.float32), -6.0, 6.0) * MODEL_DIM ** (-0.5)
    key_matrix = jnp.clip(jax.random.normal(local_key, (MODEL_DIM, KEY_VALUE_HEADS * HEAD_DIM), jnp.float32), -6.0, 6.0) * MODEL_DIM ** (-0.5)
    return (query_matrix, key_matrix)


def draw_w_query(key, part):
    return shared_weights(key)[0].astype(jnp.bfloat16)


def draw_w_key(key, part):
    return shared_weights(key)[1].astype(jnp.bfloat16)


def draw_gossip_bit(key, part):
    level_count = GOSSIP_LEVELS
    chosen = jax.random.randint(jax.random.fold_in(key, 21), (N_DP,), 0, level_count, dtype=jnp.int32)
    places = jax.random.permutation(jax.random.fold_in(key, 22), N_DP)[:level_count]
    return chosen.at[places].set(jnp.arange(level_count, dtype=jnp.int32))


def block_scale(rng, shape, shards, least, top_value):
    level, own = 1.0, jax.random.fold_in(rng, 6)
    for position, blocks in shards:
        steps = jnp.exp(jax.random.uniform(jax.random.fold_in(own, position), (blocks,), jnp.float32, least / len(shards), top_value / len(shards)))
        level = level * jnp.repeat(steps, shape[position] // blocks).reshape([-1 if axis == position else 1 for axis in range(len(shape))])
    return level


def split_up(count, total, limit, slope):
    portions = [(1 << 20) // math.isqrt(standing ** slope) + 1 for standing in range(2, count + 1)]
    spare, holding = total - limit - (count - 1), [1] * (count - 1)
    while spare > 0:
        candidates = [i for i in range(count - 1) if holding[i] < limit]
        mass, budget = sum([portions[i] for i in candidates]), spare
        for i in candidates:
            extra = min(limit - holding[i], max(1, budget * portions[i] // mass), spare)
            holding[i] = holding[i] + extra
            spare = spare - extra
    return np.array([limit] + holding)


def uneven_parts(key, count, total, bound, slope):
    if count == 2:
        one = jax.random.randint(key, (), max(1, total - bound), min(bound, total - 1) + 1)
        return jnp.stack([one, total - one])
    sizes = jnp.asarray(split_up(count, total, bound, slope), jnp.int32)
    couples = (count - 1) // 2
    donor, receiver = sizes[1:1 + 2 * couples:2], sizes[2:2 + 2 * couples:2]
    margin = jnp.minimum(donor - 1, bound - receiver)
    moved = jax.random.randint(jax.random.fold_in(key, 1), (couples,), 0, 1 << 20) % (margin + 1)
    sizes = sizes.at[1:1 + 2 * couples:2].set(donor - moved).at[2:2 + 2 * couples:2].set(receiver + moved)
    return sizes[jax.random.permutation(jax.random.fold_in(key, 2), count)]


def gaussian(stream_key, extent, spread, bound, split=(), kind=jnp.bfloat16):
    gain = block_scale(stream_key, extent, split, -0.22, 0.18) if split else 1.0
    values = jax.random.normal(stream_key, extent, jnp.float32) * spread * gain
    return jnp.minimum(jnp.maximum(values, -bound), bound).astype(kind)


def setup_inputs(seed: int = 0) -> dict:
    key_of = jax.random.split(jax.random.key(seed), 11)
    return {
        "tokens": gaussian(key_of[0], (N_DP, SEQ_DEV, LENGTH, MODEL_DIM), 1.0, 6.0, ((0, 8), (2, 4))),
        "target": gaussian(key_of[1], (N_DP, SEQ_DEV, LENGTH, MODEL_DIM), 1.0, 6.0, ((0, 8), (2, 4))),
        "rewards": jnp.clip(jnp.exp(math.log(4.0) - 2.7725887 * jax.random.uniform(key_of[2], (N_DP, SEQ_DEV, LENGTH), jnp.float32) ** block_scale(key_of[2], (N_DP, SEQ_DEV, LENGTH), ((0, 8), (2, 4)), -0.2, 0.2)), 0.25, 4.0),
        "doc_lengths": jax.vmap(lambda own: uneven_parts(own, DOCS, LENGTH, MOST_DOC, 2))(jax.random.split(key_of[3], N_DP * SEQ_DEV)).reshape((N_DP, SEQ_DEV, DOCS)).astype(jnp.int32),
        "norm_gain": jnp.clip(1.0 + 0.18 * jax.random.normal(key_of[4], (MODEL_DIM,), jnp.float32), 0.1, 1.9),
        "w_query": draw_w_query(jax.random.fold_in(key_of[10], 71), 0),
        "w_key": draw_w_key(jax.random.fold_in(key_of[10], 71), 0),
        "w_value": gaussian(key_of[7], (MODEL_DIM, KW), MODEL_DIM ** -0.5, 0.125, ((0, 32),)),
        "w_out": gaussian(key_of[8], (QW, MODEL_DIM), QW ** -0.5, 0.1875, ((0, 32),)),
        "gossip_bit": draw_gossip_bit(jax.random.fold_in(key_of[10], 71), 0),
    }


epsilon = 1e-06
masked_score = -1e+30

def norm_rows(inputs, norm_gain):
    values = inputs.astype(jnp.float32)
    power = lax.optimization_barrier(jnp.mean(values * values, axis=-1, keepdims=True))
    return (values * lax.rsqrt(power + epsilon) * norm_gain.astype(jnp.float32)).astype(jnp.bfloat16)

def doc_index(positions, lengths):
    endings = jnp.cumsum(lengths.astype(jnp.int32), axis=-1)
    return lax.optimization_barrier(jnp.sum((endings[:, None, :] <= positions[:, :, None]).astype(jnp.int32), axis=-1))

def allowed(query_pos, key_pos, lengths):
    query_doc = doc_index(query_pos, lengths)
    key_doc = doc_index(key_pos, lengths)
    distance = query_pos[:, :, None] - key_pos[:, None, :]
    same_doc = query_doc[:, :, None] == key_doc[:, None, :]
    return (key_pos[:, None, :] >= 0) & same_doc & (distance >= 0) & (distance < WINDOW)

def split_heads(query_rows, key_tile, value_tile):
    batch_count, query_length, _ = query_rows.shape
    key_length = key_tile.shape[1]
    query_heads = query_rows.astype(jnp.float32).reshape(batch_count, query_length, KEY_VALUE_HEADS, QUERY_HEADS // KEY_VALUE_HEADS, HEAD_DIM)
    key_heads = key_tile.astype(jnp.float32).reshape(batch_count, key_length, KEY_VALUE_HEADS, HEAD_DIM)
    value_heads = value_tile.astype(jnp.float32).reshape(batch_count, key_length, KEY_VALUE_HEADS, HEAD_DIM)
    return (query_heads, key_heads, value_heads)

def attend(query_rows, key_tile, value_tile, mask):
    query_heads, key_heads, value_heads = split_heads(query_rows, key_tile, value_tile)
    scores = jnp.einsum('btkgd,bskd->bkgts', query_heads, key_heads) * HEAD_DIM ** (-0.5)
    allowed_mask = mask[:, None, None, :, :]
    scores = jnp.where(allowed_mask, scores, masked_score)
    row_max = lax.optimization_barrier(jnp.max(scores, axis=-1, keepdims=True))
    raised = jnp.where(allowed_mask, jnp.exp(scores - row_max), 0.0)
    attn_probs = (raised / lax.optimization_barrier(jnp.sum(raised, axis=-1, keepdims=True))).astype(jnp.bfloat16)
    mixed_heads = jnp.einsum('bkgts,bskd->btkgd', attn_probs.astype(jnp.float32), value_heads)
    return (attn_probs, mixed_heads.reshape(query_rows.shape[0], query_rows.shape[1], QUERY_HEADS * HEAD_DIM).astype(jnp.bfloat16))

def attend_back(query_rows, key_tile, value_tile, attn_probs, blended_block, blended_gradient):
    query_heads, key_heads, value_heads = split_heads(query_rows, key_tile, value_tile)
    batch_count, query_length, _ = query_rows.shape
    key_length = key_tile.shape[1]
    gradient_heads = blended_gradient.astype(jnp.float32).reshape(batch_count, query_length, KEY_VALUE_HEADS, QUERY_HEADS // KEY_VALUE_HEADS, HEAD_DIM)
    output_heads = blended_block.astype(jnp.float32).reshape(batch_count, query_length, KEY_VALUE_HEADS, QUERY_HEADS // KEY_VALUE_HEADS, HEAD_DIM)
    prob_grads = jnp.einsum('btkgd,bskd->bkgts', gradient_heads, value_heads)
    row_dots = jnp.transpose(lax.optimization_barrier(jnp.sum(gradient_heads * output_heads, axis=-1)), (0, 2, 3, 1))[..., None]
    probs_wide = attn_probs.astype(jnp.float32)
    score_grads = (probs_wide * (prob_grads - row_dots) * HEAD_DIM ** (-0.5)).astype(jnp.bfloat16)
    score_wide = score_grads.astype(jnp.float32)
    query_gradients = jnp.einsum('bkgts,bskd->btkgd', score_wide, key_heads)
    key_gradients = jnp.einsum('bkgts,btkgd->bskd', score_wide, query_heads)
    value_gradients = jnp.einsum('bkgts,btkgd->bskd', probs_wide, gradient_heads)
    return (query_gradients.reshape(batch_count, query_length, QUERY_HEADS * HEAD_DIM).astype(jnp.bfloat16), key_gradients.reshape(batch_count, key_length, KEY_VALUE_HEADS * HEAD_DIM).astype(jnp.bfloat16), value_gradients.reshape(batch_count, key_length, KEY_VALUE_HEADS * HEAD_DIM).astype(jnp.bfloat16))

def rounded_term(partial_term):
    return lax.optimization_barrier(partial_term.astype(jnp.bfloat16)).astype(jnp.float32)

def reference(tokens, target, rewards, doc_lengths, norm_gain, w_query, w_key, w_value, w_out, gossip_bit):
    reach_blocks = WINDOW // TOK_DEV
    key_feature_width = KEY_VALUE_HEADS * HEAD_DIM
    query_width = QUERY_HEADS * HEAD_DIM
    joined_width = query_width + 2 * key_feature_width
    span_len = (reach_blocks + 1) * TOK_DEV
    grads_in = []
    grads_out = []
    for group_index in range(N_DP):
        lengths = doc_lengths[group_index]
        normed = norm_rows(tokens[group_index], norm_gain)
        flat_rows = normed.reshape(SEQ_DEV * LENGTH, MODEL_DIM)
        query_rows = jnp.dot(flat_rows, w_query, preferred_element_type=jnp.float32).astype(jnp.bfloat16).reshape(SEQ_DEV, LENGTH, query_width)
        key_all = jnp.dot(flat_rows, w_key, preferred_element_type=jnp.float32).astype(jnp.bfloat16).reshape(SEQ_DEV, LENGTH, key_feature_width)
        value_all = jnp.dot(flat_rows, w_value, preferred_element_type=jnp.float32).astype(jnp.bfloat16).reshape(SEQ_DEV, LENGTH, key_feature_width)
        leading = jnp.zeros((SEQ_DEV, reach_blocks * TOK_DEV, key_feature_width), jnp.bfloat16)
        key_padded = jnp.concatenate([leading, key_all], axis=1)
        value_padded = jnp.concatenate([leading, value_all], axis=1)
        saved_blocks = []
        mixed_parts = []
        for shard_index in range(N_CTX):
            first_pos = shard_index * TOK_DEV
            query_pos = jnp.broadcast_to(first_pos + jnp.arange(TOK_DEV, dtype=jnp.int32), (SEQ_DEV, TOK_DEV))
            key_pos = jnp.broadcast_to(first_pos - reach_blocks * TOK_DEV + jnp.arange(span_len, dtype=jnp.int32), (SEQ_DEV, span_len))
            mask = allowed(query_pos, key_pos, lengths)
            key_tile = key_padded[:, first_pos:first_pos + span_len]
            value_tile = value_padded[:, first_pos:first_pos + span_len]
            query_block = query_rows[:, first_pos:first_pos + TOK_DEV]
            attn_probs, blended_block = attend(query_block, key_tile, value_tile, mask)
            saved_blocks.append((query_block, key_tile, value_tile, attn_probs, blended_block))
            mixed_parts.append(blended_block)
        mixed_heads = jnp.concatenate(mixed_parts, axis=1)
        mixed_flat = mixed_heads.reshape(SEQ_DEV * LENGTH, query_width)
        result = tokens[group_index].reshape(-1, MODEL_DIM).astype(jnp.float32) + jnp.dot(mixed_flat, w_out, preferred_element_type=jnp.float32)
        delta_rows = (rewards[group_index].reshape(-1, 1).astype(jnp.float32) * (result - target[group_index].reshape(-1, MODEL_DIM).astype(jnp.float32))).astype(jnp.bfloat16)
        blended_gradient = jnp.dot(delta_rows, w_out.T, preferred_element_type=jnp.float32).astype(jnp.bfloat16).reshape(SEQ_DEV, LENGTH, query_width)
        key_sum = jnp.zeros((SEQ_DEV, (N_CTX + reach_blocks) * TOK_DEV, key_feature_width), jnp.float32)
        value_sum = jnp.zeros((SEQ_DEV, (N_CTX + reach_blocks) * TOK_DEV, key_feature_width), jnp.float32)
        query_parts = []
        for shard_index in range(N_CTX):
            first_pos = shard_index * TOK_DEV
            query_block, key_tile, value_tile, attn_probs, blended_block = saved_blocks[shard_index]
            grad_block = blended_gradient[:, first_pos:first_pos + TOK_DEV]
            query_gradients, key_gradients, value_gradients = attend_back(query_block, key_tile, value_tile, attn_probs, blended_block, grad_block)
            query_parts.append(query_gradients)
            key_sum = key_sum.at[:, first_pos:first_pos + span_len].add(key_gradients.astype(jnp.float32))
            value_sum = value_sum.at[:, first_pos:first_pos + span_len].add(value_gradients.astype(jnp.float32))
        key_final = key_sum[:, reach_blocks * TOK_DEV:].astype(jnp.bfloat16)
        value_final = value_sum[:, reach_blocks * TOK_DEV:].astype(jnp.bfloat16)
        joined = jnp.concatenate([jnp.concatenate(query_parts, axis=1), key_final, value_final], axis=-1)
        delta_seq = delta_rows.reshape(SEQ_DEV, LENGTH, MODEL_DIM)
        in_total = jnp.zeros((MODEL_DIM, joined_width), jnp.float32)
        out_total = jnp.zeros((query_width, MODEL_DIM), jnp.float32)
        for shard_index in range(N_CTX):
            first_pos = shard_index * TOK_DEV
            normed_block = normed[:, first_pos:first_pos + TOK_DEV].reshape(-1, MODEL_DIM)
            joined_block = joined[:, first_pos:first_pos + TOK_DEV].reshape(-1, joined_width)
            in_total = in_total + rounded_term(jnp.dot(normed_block.T, joined_block, preferred_element_type=jnp.float32))
            blended_block = mixed_heads[:, first_pos:first_pos + TOK_DEV].reshape(-1, query_width)
            delta_block = delta_seq[:, first_pos:first_pos + TOK_DEV].reshape(-1, MODEL_DIM)
            out_total = out_total + rounded_term(jnp.dot(blended_block.T, delta_block, preferred_element_type=jnp.float32))
        grads_in.append(in_total.astype(jnp.bfloat16))
        grads_out.append(out_total.astype(jnp.bfloat16))
    stacked_in = jnp.stack(grads_in)
    stacked_out = jnp.stack(grads_out)
    partner = jnp.bitwise_xor(jnp.arange(N_DP, dtype=jnp.int32), jnp.left_shift(jnp.ones((N_DP,), jnp.int32), gossip_bit.astype(jnp.int32)))
    mates_in = jnp.take(stacked_in, partner, axis=0)
    mates_out = jnp.take(stacked_out, partner, axis=0)
    mean_in = (stacked_in.astype(jnp.float32) + mates_in.astype(jnp.float32)) * 0.5
    mean_out = (stacked_out.astype(jnp.float32) + mates_out.astype(jnp.float32)) * 0.5
    return (mean_in[:, :, :query_width], mean_in[:, :, query_width:query_width + key_feature_width], mean_in[:, :, query_width + key_feature_width:], mean_out)
```

```python
import jax
import jax.numpy as jnp
from jax import lax
from jax.experimental import pallas as pl
from jax.experimental.pallas import tpu as pltpu
from jax.sharding import PartitionSpec as P

QUERY_HEADS = 4
KEY_VALUE_HEADS = 2
HEAD_DIM = 256
WINDOW = 1024


epsilon = 1e-06
masked_score = -1e30


def partner(value, axis, bit):
    mask = 2**bit
    pairs = [(source, source ^ mask) for source in range(lax.axis_size(axis))]
    return lax.ppermute(value, axis, pairs)


def shifted(block, axis, distance):
    devices = range(lax.axis_size(axis))
    route = [(i - distance, i) for i in devices if i - distance in devices]
    return lax.ppermute(block, axis, route)


def norm_rows(inputs, norm_gain):
    values = inputs.astype(jnp.float32)
    power = jnp.mean(values * values, axis=-1, keepdims=True)
    return (values * lax.rsqrt(power + epsilon) * norm_gain).astype(jnp.bfloat16)


def doc_index(positions, lengths):
    endings = jnp.cumsum(lengths, axis=-1)
    return jnp.sum((endings[:, None, :] <= positions[:, :, None]).astype(jnp.int32), axis=-1)


def allowed(query_pos, key_pos, lengths):
    query_doc = doc_index(query_pos, lengths)
    key_doc = doc_index(key_pos, lengths)
    distance = query_pos[:, :, None] - key_pos[:, None, :]
    same_doc = query_doc[:, :, None] == key_doc[:, None, :]
    return (key_pos[:, None, :] >= 0) & same_doc & (distance >= 0) & (distance < WINDOW)


def split_heads(query_rows, key_tile, value_tile):
    batch_count, query_length, _ = query_rows.shape
    key_length = key_tile.shape[1]
    query_heads = query_rows.reshape(
        batch_count, query_length, KEY_VALUE_HEADS, QUERY_HEADS // KEY_VALUE_HEADS, HEAD_DIM
    )
    key_heads = key_tile.reshape(batch_count, key_length, KEY_VALUE_HEADS, HEAD_DIM)
    value_heads = value_tile.reshape(batch_count, key_length, KEY_VALUE_HEADS, HEAD_DIM)
    return (query_heads, key_heads, value_heads)


def attend(query_rows, key_tile, value_tile, mask):
    query_heads, key_heads, value_heads = split_heads(query_rows, key_tile, value_tile)
    scores = jnp.einsum(
        "btkgd,bskd->bkgts", query_heads, key_heads, preferred_element_type=jnp.float32
    ) * HEAD_DIM ** (-0.5)
    allowed_mask = mask[:, None, None, :, :]
    scores = jnp.where(allowed_mask, scores, masked_score)
    row_max = jnp.max(scores, axis=-1, keepdims=True)
    raised = jnp.where(allowed_mask, jnp.exp(scores - row_max), 0.0)
    attn_probs = (raised / jnp.sum(raised, axis=-1, keepdims=True)).astype(jnp.bfloat16)
    mixed_heads = jnp.einsum(
        "bkgts,bskd->btkgd", attn_probs, value_heads, preferred_element_type=jnp.float32
    )
    return (
        attn_probs,
        mixed_heads.reshape(
            query_rows.shape[0], query_rows.shape[1], QUERY_HEADS * HEAD_DIM
        ).astype(jnp.bfloat16),
    )


def attend_back(query_rows, key_tile, value_tile, attn_probs, blended_block, blended_gradient):
    query_heads, key_heads, value_heads = split_heads(query_rows, key_tile, value_tile)
    batch_count, query_length, _ = query_rows.shape
    key_length = key_tile.shape[1]
    gradient_heads = blended_gradient.reshape(
        batch_count, query_length, KEY_VALUE_HEADS, QUERY_HEADS // KEY_VALUE_HEADS, HEAD_DIM
    )
    output_heads = blended_block.reshape(
        batch_count, query_length, KEY_VALUE_HEADS, QUERY_HEADS // KEY_VALUE_HEADS, HEAD_DIM
    )
    prob_grads = jnp.einsum(
        "btkgd,bskd->bkgts", gradient_heads, value_heads, preferred_element_type=jnp.float32
    )
    row_dots = jnp.sum(
        gradient_heads.astype(jnp.float32) * output_heads.astype(jnp.float32), axis=-1
    )
    row_dots = jnp.transpose(row_dots, (0, 2, 3, 1))[..., None]
    score_grads = (
        attn_probs.astype(jnp.float32) * (prob_grads - row_dots) * HEAD_DIM ** (-0.5)
    ).astype(jnp.bfloat16)
    query_gradients = jnp.einsum(
        "bkgts,bskd->btkgd", score_grads, key_heads, preferred_element_type=jnp.float32
    )
    key_gradients = jnp.einsum(
        "bkgts,btkgd->bskd", score_grads, query_heads, preferred_element_type=jnp.float32
    )
    value_gradients = jnp.einsum(
        "bkgts,btkgd->bskd", attn_probs, gradient_heads, preferred_element_type=jnp.float32
    )
    return (
        query_gradients.reshape(batch_count, query_length, QUERY_HEADS * HEAD_DIM).astype(
            jnp.bfloat16
        ),
        key_gradients.reshape(batch_count, key_length, KEY_VALUE_HEADS * HEAD_DIM).astype(
            jnp.bfloat16
        ),
        value_gradients.reshape(batch_count, key_length, KEY_VALUE_HEADS * HEAD_DIM).astype(
            jnp.bfloat16
        ),
    )


def trade(shard_pair, bit_number):
    return partner((shard_pair[0], shard_pair[1]), "dp", bit_number)


def per_device_general(
    tokens, target, rewards, doc_lengths, norm_gain, w_query, w_key, w_value, w_out, gossip_bit
):
    seq_count, shard_len, model_width = (tokens.shape[1], tokens.shape[2], tokens.shape[3])
    query_width = w_query.shape[1]
    key_feature_width = w_key.shape[1]
    row_count = seq_count * shard_len
    reach_blocks = WINDOW // shard_len
    span_len = (reach_blocks + 1) * shard_len
    ctx_index = lax.axis_index("ctx")
    lengths = doc_lengths[0]
    normed = norm_rows(tokens[0], norm_gain)
    flat_rows = normed.reshape(row_count, model_width)
    pieces = (
        lax.all_gather(w_query, ("dp", "ctx"), axis=0, tiled=True),
        lax.all_gather(w_key, ("dp", "ctx"), axis=0, tiled=True),
        lax.all_gather(w_value, ("dp", "ctx"), axis=0, tiled=True),
    )
    columns = flat_rows
    query_sum, key_sum, value_sum = tuple(
        (
            jnp.dot(columns, weight_piece, preferred_element_type=jnp.float32)
            for weight_piece in pieces
        )
    )
    query_rows = query_sum.astype(jnp.bfloat16).reshape(seq_count, shard_len, query_width)
    key_own = key_sum.astype(jnp.bfloat16).reshape(seq_count, shard_len, key_feature_width)
    value_own = value_sum.astype(jnp.bfloat16).reshape(seq_count, shard_len, key_feature_width)
    key_parts = []
    value_parts = []
    for offset in range(reach_blocks, 0, -1):
        moved = shifted((key_own, value_own), "ctx", offset)
        key_parts.append(moved[0])
        value_parts.append(moved[1])
    key_tile = jnp.concatenate(key_parts + [key_own], axis=1)
    value_tile = jnp.concatenate(value_parts + [value_own], axis=1)
    query_pos = jnp.broadcast_to(
        ctx_index * shard_len + jnp.arange(shard_len, dtype=jnp.int32), (seq_count, shard_len)
    )
    key_pos = jnp.broadcast_to(
        (ctx_index - reach_blocks) * shard_len + jnp.arange(span_len, dtype=jnp.int32),
        (seq_count, span_len),
    )
    mask = allowed(query_pos, key_pos, lengths)
    attn_probs, mixed_heads = attend(query_rows, key_tile, value_tile, mask)
    mixed_flat = mixed_heads.reshape(row_count, query_width)
    out_whole = lax.all_gather(w_out, ("dp", "ctx"), axis=0, tiled=True)
    update = jnp.dot(mixed_flat, out_whole, preferred_element_type=jnp.float32)
    result = tokens[0].reshape(row_count, model_width).astype(jnp.float32) + update
    delta_rows = (
        rewards[0].reshape(row_count, 1)
        * (result - target[0].reshape(row_count, model_width).astype(jnp.float32))
    ).astype(jnp.bfloat16)
    blended_gradient = lax.dot_general(
        delta_rows, out_whole, (((1,), (1,)), ((), ())), preferred_element_type=jnp.float32
    )
    blended_gradient = blended_gradient.astype(jnp.bfloat16).reshape(
        seq_count, shard_len, query_width
    )
    query_gradients, key_terms, value_terms = attend_back(
        query_rows, key_tile, value_tile, attn_probs, mixed_heads, blended_gradient
    )
    own_start = reach_blocks * shard_len
    key_total = key_terms[:, own_start:].astype(jnp.float32)
    value_total = value_terms[:, own_start:].astype(jnp.float32)
    for offset in range(1, reach_blocks + 1):
        low_row = (reach_blocks - offset) * shard_len
        returned = shifted(
            (
                key_terms[:, low_row : low_row + shard_len],
                value_terms[:, low_row : low_row + shard_len],
            ),
            "ctx",
            -offset,
        )
        key_total = key_total + returned[0].astype(jnp.float32)
        value_total = value_total + returned[1].astype(jnp.float32)
    key_final = key_total.astype(jnp.bfloat16)
    value_final = value_total.astype(jnp.bfloat16)
    joined = jnp.concatenate([query_gradients, key_final, value_final], axis=-1).reshape(
        row_count, query_width + 2 * key_feature_width
    )
    columns = flat_rows
    partial_term = lax.dot_general(
        columns, joined, (((0,), (0,)), ((), ())), preferred_element_type=jnp.float32
    )
    grad_inputs = lax.psum_scatter(
        lax.optimization_barrier(partial_term.astype(jnp.bfloat16))
        .astype(jnp.float32)
        .astype(jnp.bfloat16),
        "ctx",
        scatter_dimension=0,
        tiled=True,
    )
    columns = mixed_flat
    partial_term = lax.dot_general(
        columns, delta_rows, (((0,), (0,)), ((), ())), preferred_element_type=jnp.float32
    )
    grad_outputs = lax.psum_scatter(
        lax.optimization_barrier(partial_term.astype(jnp.bfloat16))
        .astype(jnp.float32)
        .astype(jnp.bfloat16),
        "ctx",
        scatter_dimension=0,
        tiled=True,
    )
    level_count = lax.axis_size("dp").bit_length() - 1
    own_bit = gossip_bit[0]
    partner_inputs = grad_inputs
    partner_outputs = grad_outputs
    for level_number in range(level_count):
        moved_pair = trade((grad_inputs, grad_outputs), level_number)
        picked = own_bit == level_number
        partner_inputs = jnp.where(picked, moved_pair[0], partner_inputs)
        partner_outputs = jnp.where(picked, moved_pair[1], partner_outputs)
    mean_inputs = (grad_inputs.astype(jnp.float32) + partner_inputs.astype(jnp.float32)) * 0.5
    mean_outputs = (grad_outputs.astype(jnp.float32) + partner_outputs.astype(jnp.float32)) * 0.5
    return (
        mean_inputs[None, :, :query_width],
        mean_inputs[None, :, query_width : query_width + key_feature_width],
        mean_inputs[None, :, query_width + key_feature_width :],
        mean_outputs[None],
    )


def swapped(value, axis, mask):
    pairs = [(source, source ^ mask) for source in range(lax.axis_size(axis))]
    return lax.ppermute(value, axis, pairs)


def place_inputs(first_block, core, blocks, masks, copy_width, fixed_width):
    count, rows, width = blocks[0].shape
    total = count * len(blocks)
    pieces = [(s, i, m) for s in range(len(blocks)) for i, m in enumerate(masks[s])]

    def kernel(scalars, *refs):
        sources, out, sems = refs[: len(blocks)], refs[len(blocks)], refs[len(blocks) + 1]
        copies = []
        for number, (s, i, m) in enumerate(pieces):
            row = pl.multiple_of((scalars[0] ^ m) * rows, 8)
            column = pl.multiple_of(scalars[1] * copy_width, 128)
            copies.append(
                pltpu.make_async_copy(
                    sources[s].at[i, :, pl.ds(column, copy_width)],
                    out.at[pl.ds(row, rows), pl.ds(0, copy_width)],
                    sems.at[2 * number],
                )
            )
            copies.append(
                pltpu.make_async_copy(
                    sources[s].at[i, :, pl.ds(width - fixed_width, fixed_width)],
                    out.at[pl.ds(row, rows), pl.ds(copy_width, fixed_width)],
                    sems.at[2 * number + 1],
                )
            )
        for copy in copies:
            copy.start()
        for copy in copies:
            copy.wait()

    return pl.pallas_call(
        kernel,
        out_shape=jax.ShapeDtypeStruct((total * rows, copy_width + fixed_width), blocks[0].dtype),
        in_specs=[pl.BlockSpec(memory_space=pltpu.SMEM)]
        + [pl.BlockSpec(memory_space=pl.ANY)] * len(blocks),
        out_specs=pl.BlockSpec(memory_space=pl.ANY),
        scratch_shapes=[pltpu.SemaphoreType.DMA((2 * total,))],
        name="place_inputs",
    )(jnp.stack([first_block, core]).astype(jnp.int32), *blocks)


def place_outputs(first_block, head, blocks, masks, per_head):
    count, rows, width = blocks[0].shape
    total = count * len(blocks)
    pieces = [(s, i, m) for s in range(len(blocks)) for i, m in enumerate(masks[s])]

    def kernel(scalars, *refs):
        sources, out, sems = refs[: len(blocks)], refs[len(blocks)], refs[len(blocks) + 1]
        copies = []
        for number, (s, i, m) in enumerate(pieces):
            block = (scalars[0] ^ m) ^ (scalars[1] * per_head)
            row = pl.multiple_of(block * rows, 8)
            copies.append(
                pltpu.make_async_copy(
                    sources[s].at[i], out.at[pl.ds(row, rows), :], sems.at[number]
                )
            )
        for copy in copies:
            copy.start()
        for copy in copies:
            copy.wait()

    return pl.pallas_call(
        kernel,
        out_shape=jax.ShapeDtypeStruct((total * rows, width), blocks[0].dtype),
        in_specs=[pl.BlockSpec(memory_space=pltpu.SMEM)]
        + [pl.BlockSpec(memory_space=pl.ANY)] * len(blocks),
        out_specs=pl.BlockSpec(memory_space=pl.ANY),
        scratch_shapes=[pltpu.SemaphoreType.DMA((total,))],
        name="place_outputs",
    )(jnp.stack([first_block, head]).astype(jnp.int32), *blocks)


def doc_of(positions, lengths):
    ending = jnp.int32(0)
    document = jnp.zeros_like(positions)
    for number in range(lengths.shape[0]):
        ending = ending + lengths[number]
        document = document + (ending <= positions).astype(jnp.int32)
    return document


def head_forward(rows, weights, mask):
    joint = jnp.dot(rows, weights, preferred_element_type=jnp.float32).astype(jnp.bfloat16)
    query = joint[:, :HEAD_DIM]
    key = joint[:, HEAD_DIM : 2 * HEAD_DIM]
    value = joint[:, 2 * HEAD_DIM :]
    scores = lax.dot_general(
        query, key, (((1,), (1,)), ((), ())), preferred_element_type=jnp.float32
    ) * HEAD_DIM ** (-0.5)
    scores = jnp.where(mask, scores, masked_score)
    row_max = jnp.max(scores, axis=-1, keepdims=True)
    raised = jnp.where(mask, jnp.exp(scores - row_max), 0.0)
    probs = (raised / jnp.sum(raised, axis=-1, keepdims=True)).astype(jnp.bfloat16)
    mixed = jnp.dot(probs, value, preferred_element_type=jnp.float32).astype(jnp.bfloat16)
    return query, key, value, probs, mixed


def head_backward(query, key, value, probs, mixed, mixed_grad):
    prob_grads = lax.dot_general(
        mixed_grad, value, (((1,), (1,)), ((), ())), preferred_element_type=jnp.float32
    )
    row_dots = jnp.sum(
        mixed_grad.astype(jnp.float32) * mixed.astype(jnp.float32), axis=-1, keepdims=True
    )
    score_grads = (
        probs.astype(jnp.float32) * (prob_grads - row_dots) * HEAD_DIM ** (-0.5)
    ).astype(jnp.bfloat16)
    query_grads = jnp.dot(score_grads, key, preferred_element_type=jnp.float32)
    over_rows = (((0,), (0,)), ((), ()))
    key_grads = lax.dot_general(score_grads, query, over_rows, preferred_element_type=jnp.float32)
    value_grads = lax.dot_general(
        probs, mixed_grad, over_rows, preferred_element_type=jnp.float32
    )
    return query_grads.astype(jnp.bfloat16), key_grads, value_grads


def reordered(value, mask, count):
    rows = value.shape[0] // count
    return jnp.concatenate([value[(j ^ mask) * rows : (j ^ mask) * rows + rows] for j in range(count)])


def natural_heads(parts, ctx_index):
    count, bit = len(parts), 1
    while bit < count:
        flip = (ctx_index & bit) != 0
        parts = [jnp.where(flip, parts[m ^ bit], parts[m]) for m in range(count)]
        bit *= 2
    return parts


def per_device_heads(
    tokens, target, rewards, doc_lengths, norm_gain, w_query, w_key, w_value, w_out, gossip_bit
):
    ctx_count = lax.axis_size("ctx")
    level_count = lax.axis_size("dp").bit_length() - 1
    ctx_index = lax.axis_index("ctx")
    block_index = lax.axis_index("dp") * ctx_count + ctx_index
    core, chip = ctx_index % 2, ctx_index // 2
    shard_len, model_width = tokens.shape[2], tokens.shape[3]
    query_half, kv_half = w_query.shape[1] // 2, w_key.shape[1] // 2
    own_tokens, own_target = tokens[0, 0], target[0, 0]
    own_bit = gossip_bit[0]
    doc_count = doc_lengths.shape[2]

    facts = jnp.concatenate([rewards[0, 0], doc_lengths[0, 0].astype(jnp.float32)])
    padded = -(-facts.shape[0] // 1024) * 1024
    facts = jnp.pad(facts, (0, padded - facts.shape[0])).reshape(8, -1)

    def chosen(options):
        picked = options[0]
        for level in range(1, level_count):
            picked = jnp.where(own_bit == level, options[level], picked)
        return picked

    facts_of = [swapped(facts, "dp", 2**level) for level in range(level_count)]
    tokens_of = [swapped(own_tokens, "dp", 2**level) for level in range(level_count)]
    later = lax.optimization_barrier((own_target, *tokens_of))
    target_of = [swapped(later[0], "dp", 2**level) for level in range(level_count)]
    mate_facts = chosen(facts_of).reshape(-1)
    mate_rewards = mate_facts[:shard_len]
    mate_lengths = mate_facts[shard_len : shard_len + doc_count].astype(jnp.int32)
    mate_tokens = chosen(list(later[1:]))
    mate_target = chosen(target_of)

    halves = [
        jnp.concatenate(
            [
                w_query[:, i * query_half : (i + 1) * query_half],
                w_key[:, i * kv_half : (i + 1) * kv_half],
                w_value[:, i * kv_half : (i + 1) * kv_half],
            ],
            axis=1,
        )
        for i in range(2)
    ]
    kept = jnp.where(chip == 0, halves[0], halves[1])
    given = jnp.where(chip == 0, halves[1], halves[0])
    blocks_in = jnp.stack([kept, swapped(given, "ctx", 2)])
    masks_in = [0, 2]
    blocks_out = w_out[None]
    masks_out = [0]
    for level in reversed(range(level_count)):
        blocks_in = jnp.concatenate([blocks_in, swapped(blocks_in, "dp", 2**level)])
        masks_in = masks_in + [m ^ (ctx_count * 2**level) for m in masks_in]
        blocks_out = jnp.concatenate([blocks_out, swapped(blocks_out, "dp", 2**level)])
        masks_out = masks_out + [m ^ (ctx_count * 2**level) for m in masks_out]
    weights_in = place_inputs(
        block_index,
        core,
        [blocks_in, swapped(blocks_in, "ctx", 1)],
        [masks_in, [m ^ 1 for m in masks_in]],
        HEAD_DIM,
        2 * kv_half,
    )
    far_out = swapped(blocks_out, "ctx", 2)
    weights_out = place_outputs(
        block_index,
        ctx_index,
        [blocks_out, far_out, swapped(blocks_out, "ctx", 1), swapped(far_out, "ctx", 1)],
        [[m ^ x for m in masks_out] for x in (0, 2, 1, 3)],
        HEAD_DIM // w_out.shape[0],
    )

    row = jnp.arange(ctx_count * shard_len, dtype=jnp.int32)
    positions = (ctx_index ^ (row // shard_len)) * shard_len + row % shard_len
    distance = positions[:, None] - positions[None, :]
    in_window = (distance >= 0) & (distance < WINDOW)

    def spread(block):
        far = swapped(block, "ctx", 2)
        return [block, swapped(block, "ctx", 1), far, swapped(far, "ctx", 1)]

    def forward(block, lengths):
        normed = jnp.concatenate([norm_rows(b, norm_gain) for b in spread(block)])
        document = doc_of(positions, lengths)
        mask = in_window & (document[:, None] == document[None, :])
        saved = head_forward(normed, weights_in, mask)
        mixed = saved[-1]
        heads = [mixed[:shard_len]] + [
            swapped(mixed[j * shard_len : (j + 1) * shard_len], "ctx", j)
            for j in range(1, ctx_count)
        ]
        return normed, saved, jnp.concatenate(heads, axis=1)

    def backward(block, goal, reward, normed, saved, mixed_rows):
        update = jnp.dot(mixed_rows, weights_out, preferred_element_type=jnp.float32)
        result = block.astype(jnp.float32) + update
        delta_rows = (reward[:, None] * (result - goal.astype(jnp.float32))).astype(jnp.bfloat16)
        grad_rows = lax.dot_general(
            delta_rows, weights_out, (((1,), (1,)), ((), ())), preferred_element_type=jnp.float32
        ).astype(jnp.bfloat16)
        mixed_grad = jnp.concatenate(
            [grad_rows[:, :HEAD_DIM]]
            + [
                swapped(grad_rows[:, j * HEAD_DIM : (j + 1) * HEAD_DIM], "ctx", j)
                for j in range(1, ctx_count)
            ]
        )
        query_grads, key_grads, value_grads = head_backward(*saved, mixed_grad)
        given = jnp.where(core == 0, value_grads, key_grads).astype(jnp.bfloat16)
        kept = jnp.where(core == 0, key_grads, value_grads)
        taken = reordered(swapped(given, "ctx", 1), 1, ctx_count).astype(jnp.float32)
        joined = jnp.concatenate([query_grads, (kept + taken).astype(jnp.bfloat16)], axis=1)
        joined_of = [reordered(v, m, ctx_count) for m, v in enumerate(spread(joined))]
        by_head = natural_heads(joined_of, ctx_index)
        columns = model_width // ctx_count
        own_columns = lax.dynamic_slice_in_dim(normed, ctx_index * columns, columns, axis=1)
        over_rows = (((0,), (0,)), ((), ()))

        def product(right):
            return lax.dot_general(
                own_columns, right, over_rows, preferred_element_type=jnp.float32
            ).astype(jnp.bfloat16)

        query_part = product(jnp.concatenate([v[:, :HEAD_DIM] for v in by_head], axis=1))
        key_part = product(jnp.concatenate([v[:, HEAD_DIM:] for v in by_head[0::2]], axis=1))
        value_part = product(jnp.concatenate([v[:, HEAD_DIM:] for v in by_head[1::2]], axis=1))
        mixed = saved[-1]
        out_total = 0.0
        for j, delta in enumerate(spread(delta_rows)):
            term = lax.dot_general(
                mixed[j * shard_len : (j + 1) * shard_len],
                delta,
                over_rows,
                preferred_element_type=jnp.float32,
            ).astype(jnp.bfloat16)
            out_total = out_total + term.astype(jnp.float32)
        return query_part, key_part, value_part, out_total.astype(jnp.bfloat16)

    own_state = forward(own_tokens, doc_lengths[0, 0])
    mate_state = forward(mate_tokens, mate_lengths)
    own_grads = backward(own_tokens, own_target, rewards[0, 0], *own_state)
    mate_grads = backward(mate_tokens, mate_target, mate_rewards, *mate_state)
    return tuple(
        ((a.astype(jnp.float32) + b.astype(jnp.float32)) * 0.5)[None]
        for a, b in zip(own_grads, mate_grads)
    )


def per_device(*arrays):
    tokens, w_query, w_out = arrays[0], arrays[5], arrays[8]
    by_heads = (
        lax.axis_size("ctx") == QUERY_HEADS == 2 * KEY_VALUE_HEADS == 4
        and lax.axis_size("dp") & (lax.axis_size("dp") - 1) == 0
        and lax.axis_size("dp") > 1
        and tokens.shape[1] == 1
        and w_query.shape[0] % 8 == 0
        and w_out.shape[0] % 8 == 0
        and HEAD_DIM % w_out.shape[0] == 0
    )
    return (per_device_heads if by_heads else per_device_general)(*arrays)


def solution(mesh):
    placed = (
        P("dp", None, "ctx", None),
        P("dp", None, "ctx", None),
        P("dp", None, "ctx"),
        P("dp", None, None),
        P(),
        P(("dp", "ctx"), None),
        P(("dp", "ctx"), None),
        P(("dp", "ctx"), None),
        P(("dp", "ctx"), None),
        P("dp"),
    )
    return jax.shard_map(
        per_device,
        mesh=mesh,
        in_specs=placed,
        out_specs=(
            P("dp", "ctx", None),
            P("dp", "ctx", None),
            P("dp", "ctx", None),
            P("dp", "ctx", None),
        ),
        check_vma=False,
    )
```

```python
import jax
import jax.numpy as jnp
from jax import lax
from jax.experimental import pallas as pl
from jax.experimental.pallas import tpu as pltpu
from jax.sharding import PartitionSpec as P

QUERY_HEADS = 4
KEY_VALUE_HEADS = 2
HEAD_DIM = 256
WINDOW = 1024


epsilon = 1e-06
masked_score = -1e30


def partner(value, axis, bit):
    mask = 2**bit
    pairs = [(source, source ^ mask) for source in range(lax.axis_size(axis))]
    return lax.ppermute(value, axis, pairs)


def shifted(block, axis, distance):
    devices = range(lax.axis_size(axis))
    route = [(i - distance, i) for i in devices if i - distance in devices]
    return lax.ppermute(block, axis, route)


def norm_rows(inputs, norm_gain):
    values = inputs.astype(jnp.float32)
    power = jnp.mean(values * values, axis=-1, keepdims=True)
    return (values * lax.rsqrt(power + epsilon) * norm_gain).astype(jnp.bfloat16)


def doc_index(positions, lengths):
    endings = jnp.cumsum(lengths, axis=-1)
    return jnp.sum((endings[:, None, :] <= positions[:, :, None]).astype(jnp.int32), axis=-1)


def allowed(query_pos, key_pos, lengths):
    query_doc = doc_index(query_pos, lengths)
    key_doc = doc_index(key_pos, lengths)
    distance = query_pos[:, :, None] - key_pos[:, None, :]
    same_doc = query_doc[:, :, None] == key_doc[:, None, :]
    return (key_pos[:, None, :] >= 0) & same_doc & (distance >= 0) & (distance < WINDOW)


def split_heads(query_rows, key_tile, value_tile):
    batch_count, query_length, _ = query_rows.shape
    key_length = key_tile.shape[1]
    query_heads = query_rows.reshape(
        batch_count, query_length, KEY_VALUE_HEADS, QUERY_HEADS // KEY_VALUE_HEADS, HEAD_DIM
    )
    key_heads = key_tile.reshape(batch_count, key_length, KEY_VALUE_HEADS, HEAD_DIM)
    value_heads = value_tile.reshape(batch_count, key_length, KEY_VALUE_HEADS, HEAD_DIM)
    return (query_heads, key_heads, value_heads)


def attend(query_rows, key_tile, value_tile, mask):
    query_heads, key_heads, value_heads = split_heads(query_rows, key_tile, value_tile)
    scores = jnp.einsum(
        "btkgd,bskd->bkgts", query_heads, key_heads, preferred_element_type=jnp.float32
    ) * HEAD_DIM ** (-0.5)
    allowed_mask = mask[:, None, None, :, :]
    scores = jnp.where(allowed_mask, scores, masked_score)
    row_max = jnp.max(scores, axis=-1, keepdims=True)
    raised = jnp.where(allowed_mask, jnp.exp(scores - row_max), 0.0)
    attn_probs = (raised / jnp.sum(raised, axis=-1, keepdims=True)).astype(jnp.bfloat16)
    mixed_heads = jnp.einsum(
        "bkgts,bskd->btkgd", attn_probs, value_heads, preferred_element_type=jnp.float32
    )
    return (
        attn_probs,
        mixed_heads.reshape(
            query_rows.shape[0], query_rows.shape[1], QUERY_HEADS * HEAD_DIM
        ).astype(jnp.bfloat16),
    )


def attend_back(query_rows, key_tile, value_tile, attn_probs, blended_block, blended_gradient):
    query_heads, key_heads, value_heads = split_heads(query_rows, key_tile, value_tile)
    batch_count, query_length, _ = query_rows.shape
    key_length = key_tile.shape[1]
    gradient_heads = blended_gradient.reshape(
        batch_count, query_length, KEY_VALUE_HEADS, QUERY_HEADS // KEY_VALUE_HEADS, HEAD_DIM
    )
    output_heads = blended_block.reshape(
        batch_count, query_length, KEY_VALUE_HEADS, QUERY_HEADS // KEY_VALUE_HEADS, HEAD_DIM
    )
    prob_grads = jnp.einsum(
        "btkgd,bskd->bkgts", gradient_heads, value_heads, preferred_element_type=jnp.float32
    )
    row_dots = jnp.sum(
        gradient_heads.astype(jnp.float32) * output_heads.astype(jnp.float32), axis=-1
    )
    row_dots = jnp.transpose(row_dots, (0, 2, 3, 1))[..., None]
    score_grads = (
        attn_probs.astype(jnp.float32) * (prob_grads - row_dots) * HEAD_DIM ** (-0.5)
    ).astype(jnp.bfloat16)
    query_gradients = jnp.einsum(
        "bkgts,bskd->btkgd", score_grads, key_heads, preferred_element_type=jnp.float32
    )
    key_gradients = jnp.einsum(
        "bkgts,btkgd->bskd", score_grads, query_heads, preferred_element_type=jnp.float32
    )
    value_gradients = jnp.einsum(
        "bkgts,btkgd->bskd", attn_probs, gradient_heads, preferred_element_type=jnp.float32
    )
    return (
        query_gradients.reshape(batch_count, query_length, QUERY_HEADS * HEAD_DIM).astype(
            jnp.bfloat16
        ),
        key_gradients.reshape(batch_count, key_length, KEY_VALUE_HEADS * HEAD_DIM).astype(
            jnp.bfloat16
        ),
        value_gradients.reshape(batch_count, key_length, KEY_VALUE_HEADS * HEAD_DIM).astype(
            jnp.bfloat16
        ),
    )


def trade(shard_pair, bit_number):
    return partner((shard_pair[0], shard_pair[1]), "dp", bit_number)


def per_device_general(
    tokens, target, rewards, doc_lengths, norm_gain, w_query, w_key, w_value, w_out, gossip_bit
):
    seq_count, shard_len, model_width = (tokens.shape[1], tokens.shape[2], tokens.shape[3])
    query_width = w_query.shape[1]
    key_feature_width = w_key.shape[1]
    row_count = seq_count * shard_len
    reach_blocks = WINDOW // shard_len
    span_len = (reach_blocks + 1) * shard_len
    ctx_index = lax.axis_index("ctx")
    lengths = doc_lengths[0]
    normed = norm_rows(tokens[0], norm_gain)
    flat_rows = normed.reshape(row_count, model_width)
    pieces = (
        lax.all_gather(w_query, ("dp", "ctx"), axis=0, tiled=True),
        lax.all_gather(w_key, ("dp", "ctx"), axis=0, tiled=True),
        lax.all_gather(w_value, ("dp", "ctx"), axis=0, tiled=True),
    )
    columns = flat_rows
    query_sum, key_sum, value_sum = tuple(
        (
            jnp.dot(columns, weight_piece, preferred_element_type=jnp.float32)
            for weight_piece in pieces
        )
    )
    query_rows = query_sum.astype(jnp.bfloat16).reshape(seq_count, shard_len, query_width)
    key_own = key_sum.astype(jnp.bfloat16).reshape(seq_count, shard_len, key_feature_width)
    value_own = value_sum.astype(jnp.bfloat16).reshape(seq_count, shard_len, key_feature_width)
    key_parts = []
    value_parts = []
    for offset in range(reach_blocks, 0, -1):
        moved = shifted((key_own, value_own), "ctx", offset)
        key_parts.append(moved[0])
        value_parts.append(moved[1])
    key_tile = jnp.concatenate(key_parts + [key_own], axis=1)
    value_tile = jnp.concatenate(value_parts + [value_own], axis=1)
    query_pos = jnp.broadcast_to(
        ctx_index * shard_len + jnp.arange(shard_len, dtype=jnp.int32), (seq_count, shard_len)
    )
    key_pos = jnp.broadcast_to(
        (ctx_index - reach_blocks) * shard_len + jnp.arange(span_len, dtype=jnp.int32),
        (seq_count, span_len),
    )
    mask = allowed(query_pos, key_pos, lengths)
    attn_probs, mixed_heads = attend(query_rows, key_tile, value_tile, mask)
    mixed_flat = mixed_heads.reshape(row_count, query_width)
    out_whole = lax.all_gather(w_out, ("dp", "ctx"), axis=0, tiled=True)
    update = jnp.dot(mixed_flat, out_whole, preferred_element_type=jnp.float32)
    result = tokens[0].reshape(row_count, model_width).astype(jnp.float32) + update
    delta_rows = (
        rewards[0].reshape(row_count, 1)
        * (result - target[0].reshape(row_count, model_width).astype(jnp.float32))
    ).astype(jnp.bfloat16)
    blended_gradient = lax.dot_general(
        delta_rows, out_whole, (((1,), (1,)), ((), ())), preferred_element_type=jnp.float32
    )
    blended_gradient = blended_gradient.astype(jnp.bfloat16).reshape(
        seq_count, shard_len, query_width
    )
    query_gradients, key_terms, value_terms = attend_back(
        query_rows, key_tile, value_tile, attn_probs, mixed_heads, blended_gradient
    )
    own_start = reach_blocks * shard_len
    key_total = key_terms[:, own_start:].astype(jnp.float32)
    value_total = value_terms[:, own_start:].astype(jnp.float32)
    for offset in range(1, reach_blocks + 1):
        low_row = (reach_blocks - offset) * shard_len
        returned = shifted(
            (
                key_terms[:, low_row : low_row + shard_len],
                value_terms[:, low_row : low_row + shard_len],
            ),
            "ctx",
            -offset,
        )
        key_total = key_total + returned[0].astype(jnp.float32)
        value_total = value_total + returned[1].astype(jnp.float32)
    key_final = key_total.astype(jnp.bfloat16)
    value_final = value_total.astype(jnp.bfloat16)
    joined = jnp.concatenate([query_gradients, key_final, value_final], axis=-1).reshape(
        row_count, query_width + 2 * key_feature_width
    )
    columns = flat_rows
    partial_term = lax.dot_general(
        columns, joined, (((0,), (0,)), ((), ())), preferred_element_type=jnp.float32
    )
    grad_inputs = lax.psum_scatter(
        lax.optimization_barrier(partial_term.astype(jnp.bfloat16))
        .astype(jnp.float32)
        .astype(jnp.bfloat16),
        "ctx",
        scatter_dimension=0,
        tiled=True,
    )
    columns = mixed_flat
    partial_term = lax.dot_general(
        columns, delta_rows, (((0,), (0,)), ((), ())), preferred_element_type=jnp.float32
    )
    grad_outputs = lax.psum_scatter(
        lax.optimization_barrier(partial_term.astype(jnp.bfloat16))
        .astype(jnp.float32)
        .astype(jnp.bfloat16),
        "ctx",
        scatter_dimension=0,
        tiled=True,
    )
    level_count = lax.axis_size("dp").bit_length() - 1
    own_bit = gossip_bit[0]
    partner_inputs = grad_inputs
    partner_outputs = grad_outputs
    for level_number in range(level_count):
        moved_pair = trade((grad_inputs, grad_outputs), level_number)
        picked = own_bit == level_number
        partner_inputs = jnp.where(picked, moved_pair[0], partner_inputs)
        partner_outputs = jnp.where(picked, moved_pair[1], partner_outputs)
    mean_inputs = (grad_inputs.astype(jnp.float32) + partner_inputs.astype(jnp.float32)) * 0.5
    mean_outputs = (grad_outputs.astype(jnp.float32) + partner_outputs.astype(jnp.float32)) * 0.5
    return (
        mean_inputs[None, :, :query_width],
        mean_inputs[None, :, query_width : query_width + key_feature_width],
        mean_inputs[None, :, query_width + key_feature_width :],
        mean_outputs[None],
    )


def swapped(value, axis, mask):
    pairs = [(source, source ^ mask) for source in range(lax.axis_size(axis))]
    return lax.ppermute(value, axis, pairs)


def after(value, *others):
    return lax.optimization_barrier((value, *others))[0]


def place_inputs(first_block, core, blocks, masks, copy_width, fixed_width):
    count, rows, width = blocks[0].shape
    total = count * len(blocks)
    pieces = [(s, i, m) for s in range(len(blocks)) for i, m in enumerate(masks[s])]

    def kernel(scalars, *refs):
        sources, out, sems = refs[: len(blocks)], refs[len(blocks)], refs[len(blocks) + 1]
        copies = []
        for number, (s, i, m) in enumerate(pieces):
            row = pl.multiple_of((scalars[0] ^ m) * rows, 8)
            column = pl.multiple_of(scalars[1] * copy_width, 128)
            copies.append(
                pltpu.make_async_copy(
                    sources[s].at[i, :, pl.ds(column, copy_width)],
                    out.at[pl.ds(row, rows), pl.ds(0, copy_width)],
                    sems.at[2 * number],
                )
            )
            copies.append(
                pltpu.make_async_copy(
                    sources[s].at[i, :, pl.ds(width - fixed_width, fixed_width)],
                    out.at[pl.ds(row, rows), pl.ds(copy_width, fixed_width)],
                    sems.at[2 * number + 1],
                )
            )
        for copy in copies:
            copy.start()
        for copy in copies:
            copy.wait()

    return pl.pallas_call(
        kernel,
        out_shape=jax.ShapeDtypeStruct((total * rows, copy_width + fixed_width), blocks[0].dtype),
        in_specs=[pl.BlockSpec(memory_space=pltpu.SMEM)]
        + [pl.BlockSpec(memory_space=pl.ANY)] * len(blocks),
        out_specs=pl.BlockSpec(memory_space=pltpu.VMEM),
        scratch_shapes=[pltpu.SemaphoreType.DMA((2 * total,))],
        name="place_inputs",
    )(jnp.stack([first_block, core]).astype(jnp.int32), *blocks)


def place_outputs(first_block, head, blocks, masks, per_head):
    rows, width = blocks[0].shape[1:]
    pieces = [(s, i, m) for s in range(len(blocks)) for i, m in enumerate(masks[s])]
    total = len(pieces)

    def kernel(scalars, *refs):
        sources, out, sems = refs[: len(blocks)], refs[len(blocks)], refs[len(blocks) + 1]
        copies = []
        for number, (s, i, m) in enumerate(pieces):
            block = (scalars[0] ^ m) ^ (scalars[1] * per_head)
            row = pl.multiple_of(block * rows, 8)
            copies.append(
                pltpu.make_async_copy(
                    sources[s].at[i], out.at[pl.ds(row, rows), :], sems.at[number]
                )
            )
        for copy in copies:
            copy.start()
        for copy in copies:
            copy.wait()

    return pl.pallas_call(
        kernel,
        out_shape=jax.ShapeDtypeStruct((total * rows, width), blocks[0].dtype),
        in_specs=[pl.BlockSpec(memory_space=pltpu.SMEM)]
        + [pl.BlockSpec(memory_space=pl.ANY)] * len(blocks),
        out_specs=pl.BlockSpec(memory_space=pltpu.VMEM),
        scratch_shapes=[pltpu.SemaphoreType.DMA((total,))],
        name="place_outputs",
    )(jnp.stack([first_block, head]).astype(jnp.int32), *blocks)


def positions_of(head, block, shape, dimension, shard_len):
    at = lax.broadcasted_iota(jnp.int32, shape, dimension) + block * shard_len
    return jnp.bitwise_xor(head, at // shard_len) * shard_len + at % shard_len


def head_forward(rows, weights, facts, shard_len):
    length, width = rows.shape
    columns = weights.shape[1]
    blocks = length // shard_len
    scale = HEAD_DIM ** (-0.5)

    def kernel(facts_ref, rows_ref, weights_ref, joint_ref, probs_ref, mixed_ref, joint):
        phase, step = pl.program_id(0), pl.program_id(1)
        here = pl.ds(pl.multiple_of(step * shard_len, shard_len), shard_len)

        @pl.when(phase == 0)
        def _():
            product = jnp.dot(
                rows_ref[...], weights_ref[...], preferred_element_type=jnp.float32
            ).astype(jnp.bfloat16)
            joint[here, :] = product
            joint_ref[...] = product

        @pl.when(phase == 1)
        def _():
            scores = (
                lax.dot_general(
                    joint[here, :HEAD_DIM],
                    joint[:, HEAD_DIM : 2 * HEAD_DIM],
                    (((1,), (1,)), ((), ())),
                    preferred_element_type=jnp.float32,
                )
                * scale
            )
            query_pos = positions_of(facts_ref[0], step, (shard_len, 1), 0, shard_len)
            key_pos = positions_of(facts_ref[0], 0, (1, length), 1, shard_len)
            query_doc = jnp.zeros_like(query_pos)
            key_doc = jnp.zeros_like(key_pos)
            for number in range(1, facts_ref.shape[0]):
                query_doc += (facts_ref[number] <= query_pos).astype(jnp.int32)
                key_doc += (facts_ref[number] <= key_pos).astype(jnp.int32)
            distance = query_pos - key_pos
            mask = (query_doc == key_doc) & (distance >= 0) & (distance < WINDOW)
            scores = jnp.where(mask, scores, masked_score)
            row_max = jnp.max(scores, axis=-1, keepdims=True)
            raised = jnp.where(mask, jnp.exp(scores - row_max), 0.0)
            probs = (raised / jnp.sum(raised, axis=-1, keepdims=True)).astype(jnp.bfloat16)
            probs_ref[...] = probs
            mixed_ref[...] = jnp.dot(
                probs, joint[:, 2 * HEAD_DIM :], preferred_element_type=jnp.float32
            ).astype(jnp.bfloat16)

    first = lambda p, i, s: (i * (1 - p) + (blocks - 1) * p, 0)
    second = lambda p, i, s: (i * p, 0)
    return pl.pallas_call(
        kernel,
        grid_spec=pltpu.PrefetchScalarGridSpec(
            num_scalar_prefetch=1,
            grid=(2, blocks),
            in_specs=[
                pl.BlockSpec((shard_len, width), first),
                pl.BlockSpec((width, columns), lambda p, i, s: (0, 0)),
            ],
            out_specs=[
                pl.BlockSpec((shard_len, columns), first),
                pl.BlockSpec((shard_len, length), second),
                pl.BlockSpec((shard_len, HEAD_DIM), second),
            ],
            scratch_shapes=[pltpu.VMEM((length, columns), jnp.bfloat16)],
        ),
        out_shape=[
            jax.ShapeDtypeStruct((length, columns), jnp.bfloat16),
            jax.ShapeDtypeStruct((length, length), jnp.bfloat16),
            jax.ShapeDtypeStruct((length, HEAD_DIM), jnp.bfloat16),
        ],
        name="head_forward",
    )(facts, rows, weights)


def head_backward(core, joint, probs, mixed, mixed_grads, shard_len):
    length, columns = joint.shape
    blocks = length // shard_len
    scale = HEAD_DIM ** (-0.5)
    over_rows = (((0,), (0,)), ((), ()))

    def kernel(core_ref, joint_ref, probs_ref, mixed_ref, *refs):
        grad_refs, (query_ref, kept_ref, given_ref, key_sum, value_sum) = refs[:blocks], refs[blocks:]
        step = pl.program_id(0)
        here = pl.ds(pl.multiple_of(step * shard_len, shard_len), shard_len)

        @pl.when(step == 0)
        def _():
            key_sum[...] = jnp.zeros_like(key_sum)
            value_sum[...] = jnp.zeros_like(value_sum)

        for block in range(blocks):

            @pl.when(step == block)
            def _():
                grad = grad_refs[block][...]
                probs = probs_ref[...]
                prob_grads = lax.dot_general(
                    grad,
                    joint_ref[:, 2 * HEAD_DIM :],
                    (((1,), (1,)), ((), ())),
                    preferred_element_type=jnp.float32,
                )
                row_dots = jnp.sum(
                    grad.astype(jnp.float32) * mixed_ref[...].astype(jnp.float32),
                    axis=-1,
                    keepdims=True,
                )
                score_grads = (
                    probs.astype(jnp.float32) * (prob_grads - row_dots) * scale
                ).astype(jnp.bfloat16)
                query_ref[...] = jnp.dot(
                    score_grads,
                    joint_ref[:, HEAD_DIM : 2 * HEAD_DIM],
                    preferred_element_type=jnp.float32,
                ).astype(jnp.bfloat16)
                key_sum[...] += lax.dot_general(
                    score_grads,
                    joint_ref[here, :HEAD_DIM],
                    over_rows,
                    preferred_element_type=jnp.float32,
                )
                value_sum[...] += lax.dot_general(
                    probs, grad, over_rows, preferred_element_type=jnp.float32
                )

        @pl.when(step == blocks - 1)
        def _():
            keeps_key = core_ref[0] == 0
            kept_ref[...] = jnp.where(keeps_key, key_sum[...], value_sum[...])
            given_ref[...] = jnp.where(keeps_key, value_sum[...], key_sum[...]).astype(jnp.bfloat16)

    whole = lambda i, s: (0, 0)
    return pl.pallas_call(
        kernel,
        grid_spec=pltpu.PrefetchScalarGridSpec(
            num_scalar_prefetch=1,
            grid=(blocks,),
            in_specs=[
                pl.BlockSpec((length, columns), whole),
                pl.BlockSpec((shard_len, length), lambda i, s: (i, 0)),
                pl.BlockSpec((shard_len, HEAD_DIM), lambda i, s: (i, 0)),
            ]
            + [pl.BlockSpec((shard_len, HEAD_DIM), whole)] * blocks,
            out_specs=[
                pl.BlockSpec((shard_len, HEAD_DIM), lambda i, s: (i, 0)),
                pl.BlockSpec((length, HEAD_DIM), whole),
                pl.BlockSpec((length, HEAD_DIM), whole),
            ],
            scratch_shapes=[pltpu.VMEM((length, HEAD_DIM), jnp.float32)] * 2,
        ),
        out_shape=[
            jax.ShapeDtypeStruct((length, HEAD_DIM), jnp.bfloat16),
            jax.ShapeDtypeStruct((length, HEAD_DIM), jnp.float32),
            jax.ShapeDtypeStruct((length, HEAD_DIM), jnp.bfloat16),
        ],
        name="head_backward",
    )(core[None].astype(jnp.int32), joint, probs, mixed, *mixed_grads)


def input_grads(head, normed, joined_of, earlier, shard_len):
    length, width = normed.shape
    count = len(joined_of)
    rows = width // count
    blocks = length // shard_len
    order = [0, 2, 1, 3]
    kind = jnp.bfloat16 if earlier is None else jnp.float32
    over_rows = (((0,), (0,)), ((), ()))

    def source(step, scalars):
        mask = jnp.where(step == 1, 2, jnp.where(step == 2, 1, step))
        return jnp.bitwise_xor(scalars[0], mask)

    def query_at(step, scalars):
        return (0, source(step, scalars))

    def pair_at(bit):
        def at(step, scalars):
            first = scalars[0] % 2 == bit
            shown = jnp.where(first, jnp.minimum(step, 1), jnp.maximum(step, 2))
            return (0, source(shown, scalars) // 2)

        return at

    def kernel(scalars, normed_ref, *refs):
        joined_refs = refs[:count]
        earlier_refs = refs[count : len(refs) - 4]
        outs, turned = refs[len(refs) - 4 : len(refs) - 1], refs[len(refs) - 1]
        step = pl.program_id(0)

        @pl.when(step == 0)
        def _():
            turned[...] = normed_ref[...].T

        def store(number, value):
            value = value.astype(jnp.bfloat16)
            if earlier_refs:
                value = value.astype(jnp.float32) + earlier_refs[number][...].astype(jnp.float32)
                value = value * 0.5
            outs[number][...] = value

        for number, mask in enumerate(order):

            @pl.when(step == number)
            def _():
                total = None
                for block in range(blocks):
                    low = (block ^ mask) * shard_len
                    term = jnp.dot(
                        turned[:, block * shard_len : (block + 1) * shard_len],
                        joined_refs[mask][low : low + shard_len, :],
                        preferred_element_type=jnp.float32,
                    )
                    total = term if total is None else total + term
                store(0, total[:, :HEAD_DIM])
                bit = jnp.bitwise_xor(scalars[0], mask) % 2

                @pl.when(bit == 0)
                def _():
                    store(1, total[:, HEAD_DIM:])

                @pl.when(bit == 1)
                def _():
                    store(2, total[:, HEAD_DIM:])

    tiles = [
        pl.BlockSpec((rows, HEAD_DIM), query_at),
        pl.BlockSpec((rows, HEAD_DIM), pair_at(0)),
        pl.BlockSpec((rows, HEAD_DIM), pair_at(1)),
    ]
    widths = [count * HEAD_DIM, count // 2 * HEAD_DIM, count // 2 * HEAD_DIM]
    return pl.pallas_call(
        kernel,
        grid_spec=pltpu.PrefetchScalarGridSpec(
            num_scalar_prefetch=1,
            grid=(count,),
            in_specs=[pl.BlockSpec((length, rows), lambda i, s: (0, s[0]))]
            + [pl.BlockSpec((length, 2 * HEAD_DIM), lambda i, s: (0, 0))] * count
            + ([] if earlier is None else tiles),
            out_specs=tiles,
            scratch_shapes=[pltpu.VMEM((rows, length), jnp.bfloat16)],
        ),
        out_shape=[jax.ShapeDtypeStruct((rows, w), kind) for w in widths],
        name="input_grads",
    )(head[None].astype(jnp.int32), normed, *joined_of, *(earlier or ()))


def per_device_heads(
    tokens, target, rewards, doc_lengths, norm_gain, w_query, w_key, w_value, w_out, gossip_bit
):
    ctx_count = lax.axis_size("ctx")
    level_count = lax.axis_size("dp").bit_length() - 1
    ctx_index = lax.axis_index("ctx")
    block_index = lax.axis_index("dp") * ctx_count + ctx_index
    core, chip = ctx_index % 2, ctx_index // 2
    shard_len = tokens.shape[2]
    query_half, kv_half = w_query.shape[1] // 2, w_key.shape[1] // 2
    own_tokens, own_target = tokens[0, 0], target[0, 0]
    own_bit = gossip_bit[0]
    doc_count = doc_lengths.shape[2]
    levels = range(level_count)

    facts = jnp.concatenate([rewards[0, 0], doc_lengths[0, 0].astype(jnp.float32)])
    padded = -(-facts.shape[0] // 1024) * 1024
    facts = jnp.pad(facts, (0, padded - facts.shape[0])).reshape(8, -1)

    halves = [
        jnp.concatenate(
            [
                w_query[:, i * query_half : (i + 1) * query_half],
                w_key[:, i * kv_half : (i + 1) * kv_half],
                w_value[:, i * kv_half : (i + 1) * kv_half],
            ],
            axis=1,
        )
        for i in range(2)
    ]
    kept = jnp.where(chip == 0, halves[0], halves[1])
    given = jnp.where(chip == 0, halves[1], halves[0])
    moved = swapped(given, "ctx", 2)
    blocks_in = jnp.stack([kept, moved])
    masks_in = [0, 2]
    blocks_out = w_out[None]
    masks_out = [0]
    held_out = []
    tokens_of, target_of, facts_of = {}, {}, {}
    for level in levels:
        facts_of[level] = swapped(facts, "dp", 2**level)
    for level in range(level_count - 1):
        tokens_of[level] = swapped(own_tokens, "dp", 2**level)
    own_far = swapped(after(own_tokens, moved), "ctx", 2)
    for level in reversed(levels):
        last = level == 0
        moved = swapped(blocks_in, "dp", 2**level)
        if last:
            top = level_count - 1
            tokens_of[top] = swapped(after(own_tokens, blocks_in), "dp", 2**top)
            for other in range(1, top):
                target_of[other] = swapped(
                    after(own_target, blocks_in, tokens_of[other]), "dp", 2**other
                )
        blocks_in = jnp.concatenate([blocks_in, moved])
        masks_in = masks_in + [m ^ (ctx_count * 2**level) for m in masks_in]
        moved_out = swapped(after(blocks_out, moved), "dp", 2**level)
        if last:
            held_out = [(blocks_out, masks_out)]
            held_out.append((moved_out, [m ^ (ctx_count * 2**level) for m in masks_out]))
        else:
            blocks_out = jnp.concatenate([blocks_out, moved_out])
            masks_out = masks_out + [m ^ (ctx_count * 2**level) for m in masks_out]
    target_of[0] = swapped(after(own_target, moved_out, tokens_of[0]), "dp", 1)
    top = level_count - 1
    if top > 0:
        target_of[top] = swapped(after(own_target, tokens_of[top]), "dp", 2**top)
    weights_in = place_inputs(
        block_index,
        core,
        [blocks_in, swapped(blocks_in, "ctx", 1)],
        [masks_in, [m ^ 1 for m in masks_in]],
        HEAD_DIM,
        2 * kv_half,
    )
    held_out += [(swapped(v, "ctx", 2), [m ^ 2 for m in masks]) for v, masks in held_out]
    held_out += [(swapped(v, "ctx", 1), [m ^ 1 for m in masks]) for v, masks in held_out]
    weights_out = place_outputs(
        block_index,
        ctx_index,
        [v for v, _ in held_out],
        [masks for _, masks in held_out],
        HEAD_DIM // w_out.shape[0],
    )

    def chosen(options):
        picked = options[0]
        for level in range(1, level_count):
            picked = jnp.where(own_bit == level, options[level], picked)
        return picked

    mate_facts = chosen(facts_of).reshape(-1)
    mate_rewards = mate_facts[:shard_len]
    mate_lengths = mate_facts[shard_len : shard_len + doc_count].astype(jnp.int32)
    mate_tokens = chosen(tokens_of)
    mate_target = chosen(target_of)
    mate_far = swapped(mate_tokens, "ctx", 2)

    def facts_for(lengths):
        ends = [ctx_index, lengths[0]]
        for number in range(1, doc_count):
            ends.append(ends[-1] + lengths[number])
        return jnp.stack(ends).astype(jnp.int32)

    def spread(block, far=None):
        far = swapped(block, "ctx", 2) if far is None else far
        return [block, swapped(block, "ctx", 1), far, swapped(far, "ctx", 1)]

    def forward(block, far, lengths):
        normed = jnp.concatenate([norm_rows(b, norm_gain) for b in spread(block, far)])
        joint, probs, mixed = head_forward(normed, weights_in, facts_for(lengths), shard_len)
        heads = [mixed[:shard_len]] + [
            swapped(mixed[j * shard_len : (j + 1) * shard_len], "ctx", j)
            for j in range(1, ctx_count)
        ]
        return normed, (joint, probs, mixed), jnp.concatenate(heads, axis=1)

    def backward(block, goal, reward, normed, saved, mixed_rows, earlier):
        update = jnp.dot(mixed_rows, weights_out, preferred_element_type=jnp.float32)
        result = block.astype(jnp.float32) + update
        delta_rows = (reward[:, None] * (result - goal.astype(jnp.float32))).astype(jnp.bfloat16)
        grad_rows = lax.dot_general(
            delta_rows, weights_out, (((1,), (1,)), ((), ())), preferred_element_type=jnp.float32
        ).astype(jnp.bfloat16)
        mixed_grads = [grad_rows[:, :HEAD_DIM]] + [
            swapped(grad_rows[:, j * HEAD_DIM : (j + 1) * HEAD_DIM], "ctx", j)
            for j in range(1, ctx_count)
        ]
        query_grads, kept, given = head_backward(core, *saved, mixed_grads, shard_len)
        taken = swapped(given, "ctx", 1).astype(jnp.float32)
        taken = jnp.concatenate(
            [taken[(j ^ 1) * shard_len : ((j ^ 1) + 1) * shard_len] for j in range(ctx_count)]
        )
        joined = jnp.concatenate([query_grads, (kept + taken).astype(jnp.bfloat16)], axis=1)
        grads = input_grads(ctx_index, normed, spread(joined), earlier, shard_len)
        return grads, delta_rows, mixed_grads

    own_state = forward(own_tokens, own_far, doc_lengths[0, 0])
    mate_state = forward(mate_tokens, mate_far, mate_lengths)
    own_grads, own_delta, _ = backward(
        own_tokens, own_target, rewards[0, 0], *own_state, None
    )
    grads, mate_delta, mate_mixed_grads = backward(
        mate_tokens, mate_target, mate_rewards, *mate_state, own_grads
    )

    over_rows = (((0,), (0,)), ((), ()))
    terms = sum(
        lax.dot_general(a, b, over_rows, preferred_element_type=jnp.float32)
        for a, b in ((own_state[2], own_delta), (mate_state[2], mate_delta))
    )
    parts = [terms[j * HEAD_DIM : (j + 1) * HEAD_DIM] for j in range(ctx_count)]
    near = jnp.concatenate([parts[1], parts[3]]).astype(jnp.bfloat16)
    near = swapped(after(near, *mate_mixed_grads), "ctx", 1).astype(jnp.float32)
    here = parts[0] + near[:HEAD_DIM]
    there = (parts[2] + near[HEAD_DIM:]).astype(jnp.bfloat16)
    grad_out = (here + swapped(there, "ctx", 2).astype(jnp.float32)) * 0.5
    return tuple(g[None] for g in (*grads, grad_out))


def per_device(*arrays):
    tokens, w_query, w_out = arrays[0], arrays[5], arrays[8]
    by_heads = (
        lax.axis_size("ctx") == QUERY_HEADS == 2 * KEY_VALUE_HEADS == 4
        and lax.axis_size("dp") & (lax.axis_size("dp") - 1) == 0
        and lax.axis_size("dp") > 1
        and tokens.shape[1] == 1
        and w_query.shape[0] % 8 == 0
        and w_out.shape[0] % 8 == 0
        and HEAD_DIM % w_out.shape[0] == 0
    )
    return (per_device_heads if by_heads else per_device_general)(*arrays)


def solution(mesh):
    placed = (
        P("dp", None, "ctx", None),
        P("dp", None, "ctx", None),
        P("dp", None, "ctx"),
        P("dp", None, None),
        P(),
        P(("dp", "ctx"), None),
        P(("dp", "ctx"), None),
        P(("dp", "ctx"), None),
        P(("dp", "ctx"), None),
        P("dp"),
    )
    return jax.shard_map(
        per_device,
        mesh=mesh,
        in_specs=placed,
        out_specs=(
            P("dp", "ctx", None),
            P("dp", "ctx", None),
            P("dp", "ctx", None),
            P("dp", "ctx", None),
        ),
        check_vma=False,
    )
```
